32 devices in a mesh: gx: 8 (over y, x, core), gy: 4 (over z).
Axes of the slice: x: 2, y: 2, z: 4, core: 2. Of those that a mesh axis runs over, the one named last changes fastest.
Arguments:
- support_funcs: bfloat16 [3072, 16, 128], P('gx', 'gy'), may hold values from -6 to 6
- potential: float32 [16, 128], P('gy'), may hold values from -1 to 1
- kernel: bfloat16 [4, 48, 64, 64], P('gy', 'gx'), may hold values from -0.375 to 0.375
- weighted: bfloat16 [4, 48, 64, 64], P('gy', 'gx'), may hold values from -0.375 to 0.375
- columns: int32 [48, 4], P('gx'), may hold values from 0 to 47, as said below
- regions: int32 [48, 4], P('gx'), may hold values from 0 to 128, as said below
Outputs:
- new_support: float32 [3072, 16, 128], P('gx', 'gy')
- hamiltonian: float32 [4, 48, 64, 64], P('gy', 'gx')
The draws below stay inside these ranges and needn't reach their ends.
Inputs may be any that keep to these rules, and one draw needn't show every extreme that they name: `columns`: the column blocks of row block a are 4 distinct blocks among the 18 blocks owned by gx index a // 6 and its two neighbours, counted cyclically. `regions`: every box spans at least half of 16 along y and half of 128 along z; it starts at 0 in both dimensions where the block index is even and ends at 16 and 128 where it is odd.
All inputs are finite; a program needn't handle non-finite values.
Results may differ from the reference program's by a relative error of at most 0.0011.
Values may be sent and summed in bfloat16 or wider, within the bound.
A program may use at most 64 MiB of HBM per device.

```python
import jax
import jax.numpy as jnp
from jax import lax

B = 64
NBG = 6
CZ = 128
SWEEPS = 3
NB = 48
NORB = 3072
NNZ = 4
NY = 16


def draw_columns(key, part):
    owner_count = NB // NBG
    rows = jnp.arange(NB, dtype=jnp.int32)
    owner = rows // NBG
    keys = jax.random.split(jax.random.fold_in(key, 11), NB)
    picks = jax.vmap(lambda k: jax.random.permutation(k, 3 * NBG))(keys)[:, :NNZ].astype(jnp.int32)
    col_owner = (owner[:, None] - 1 + picks // NBG + owner_count) % owner_count
    return (col_owner * NBG + picks % NBG).astype(jnp.int32)


def draw_regions(key, part):
    key_y, key_z = jax.random.split(jax.random.fold_in(key, 23))
    len_y = jax.random.randint(key_y, (NB,), NY // 2, NY + 1).astype(jnp.int32)
    len_z = jax.random.randint(key_z, (NB,), CZ // 2, CZ + 1).astype(jnp.int32)
    parity = jnp.arange(NB, dtype=jnp.int32) % 2 == 1
    y_from = jnp.where(parity, NY - len_y, 0)
    y_to = jnp.where(parity, NY, len_y)
    z_from = jnp.where(parity, CZ - len_z, 0)
    z_to = jnp.where(parity, CZ, len_z)
    return jnp.stack([y_from, y_to, z_from, z_to], axis=1).astype(jnp.int32)


def levels(key, shape, pieces, smallest, largest):
    level = 1.0
    for axis_at, blocks in pieces:
        heights = jax.random.uniform(jax.random.fold_in(jax.random.fold_in(key, 6), axis_at), (blocks,), jnp.float32, smallest / len(pieces), largest / len(pieces))
        level = level * jnp.repeat(jnp.exp(heights), shape[axis_at] // blocks).reshape((-1,) + (1,) * (len(shape) - 1 - axis_at))
    return level


def normal_values(key, extent, spread, bound, cuts=(), kind=jnp.bfloat16):
    drawn = jax.random.normal(key, extent, jnp.float32) * spread
    if len(cuts) > 0:
        drawn = levels(key, extent, cuts, -0.22, 0.18) * drawn
    return jnp.clip(drawn, min=-bound, max=bound).astype(kind)


def setup_inputs(seed: int = 0) -> dict:
    splits = jax.random.split(jax.random.key(seed), 7)
    support_funcs = normal_values(splits[0], (NORB, NY, CZ), 1.0, 6.0, ((0, 8), (1, 4)))
    potential = jnp.clip(jax.random.uniform(splits[1], (NY, CZ), jnp.float32, -1.0, 1.0) * levels(splits[1], (NY, CZ), ((0, 4),), -0.4, 0.0), -1.0, 1.0)
    kernel = normal_values(splits[2], (NNZ, NB, B, B), (B * NNZ) ** -0.5, 0.375, ((0, 4), (1, 8)))
    weighted = normal_values(splits[3], (NNZ, NB, B, B), (B * NNZ) ** -0.5, 0.375, ((0, 4), (1, 8)))
    columns = draw_columns(jax.random.fold_in(splits[6], 71), 0)
    regions = draw_regions(jax.random.fold_in(splits[6], 71), 0)
    return {"support_funcs": support_funcs, "potential": potential, "kernel": kernel, "weighted": weighted, "columns": columns, "regions": regions}


kinetic_cut = 1.0
step_length = 0.5


def apply_ham(field, potential):
    padded = jnp.pad(field, ((0, 0), (1, 1), (0, 0)))
    beside = padded[:, 2:] + padded[:, :-2] + jnp.roll(field, 1, 2) + jnp.roll(field, -1, 2)
    return -0.5 * (beside - 4.0 * field) + potential[None] * field


def precondition(gradient):
    diag = 1.0 + 2.0 / kinetic_cut
    coef = 0.5 / kinetic_cut
    precond = gradient / diag
    for sweep in range(SWEEPS):
        padded = jnp.pad(precond, ((0, 0), (1, 1), (0, 0)))
        beside = padded[:, 2:] + padded[:, :-2] + jnp.roll(precond, 1, 2) + jnp.roll(precond, -1, 2)
        precond = (gradient + coef * beside) / diag
    return precond


def reference(support_funcs, potential, kernel, weighted, columns, regions):
    phi = support_funcs.astype(jnp.float32)
    applied = apply_ham(phi, potential).astype(jnp.bfloat16)
    cells = NY * CZ
    volume = 1.0 / cells
    applied_blocks = applied.reshape(NB, B, cells)
    phi_blocks = support_funcs.reshape(NB, B, cells)

    def one_row(row):
        picked = columns[row]
        applied_sel = applied_blocks[picked].astype(jnp.float32)
        phi_sel = phi_blocks[picked].astype(jnp.float32)
        kern_rows = kernel[:, row].astype(jnp.float32)
        wght_rows = weighted[:, row].astype(jnp.float32)
        grad_row = jnp.einsum('kij,kjr->ir', kern_rows, applied_sel, precision=lax.Precision.HIGHEST) - jnp.einsum('kij,kjr->ir', wght_rows, phi_sel, precision=lax.Precision.HIGHEST)
        own_block = phi_blocks[row].astype(jnp.float32)
        ham_row = jnp.einsum('ir,kjr->kij', own_block, applied_sel, precision=lax.Precision.HIGHEST) * volume
        return grad_row, ham_row

    grads, hams = lax.map(one_row, jnp.arange(NB, dtype=jnp.int32))
    gradient = grads.reshape(NB * B, NY, CZ)
    precond = precondition(gradient)
    y_index = jnp.arange(NY, dtype=jnp.int32)[None, :, None]
    z_index = jnp.arange(CZ, dtype=jnp.int32)[None, None, :]
    inside = (y_index >= regions[:, 0, None, None]) & (y_index < regions[:, 1, None, None]) & (z_index >= regions[:, 2, None, None]) & (z_index < regions[:, 3, None, None])
    inside = jnp.repeat(inside.astype(jnp.float32), B, axis=0)
    new_support = phi - step_length * (inside * precond)
    return new_support, jnp.transpose(hams, (1, 0, 2, 3))
```

```python
import functools

import jax
import jax.numpy as jnp
from jax import lax
from jax.experimental import pallas as pl
from jax.experimental.pallas import tpu as pltpu
from jax.sharding import PartitionSpec as P

SWEEPS = 3
CHUNK = 2
kinetic_cut = 1.0
step_length = 0.5
f32 = jnp.float32
bf16 = jnp.bfloat16


def remote(src, dst, send, recv, **device):
    return pltpu.make_async_remote_copy(
        src_ref=src,
        dst_ref=dst,
        send_sem=send,
        recv_sem=recv,
        device_id=device,
        device_id_type=pl.DeviceIdType.MESH,
    )


def loop(count, body):
    def step(i, carry):
        body(i)
        return carry

    lax.fori_loop(0, count, step, 0)


def kernel_body(
    n_gx, n_gy, rows_y,
    cols_ref, regs_ref, pot_ref, x_ref, kern_ref, wght_ref,
    out_ref, ham_ref,
    raw, wide, near_phi, near_app, edge_send, edge_recv, pack, packs,
    grad, halo_send, halo_recv, part, part_recv,
    x_send, x_recv, e_send, e_recv, k_send, k_recv, k_own, g_send, g_recv, h_send, h_recv,
):
    gx, gy = lax.axis_index("gx"), lax.axis_index("gy")
    right, left = lax.rem(gx + 1, n_gx), lax.rem(gx + n_gx - 1, n_gx)
    own_slots, nb, size = kern_ref.shape[:3]
    slots = own_slots * n_gy
    depth = x_ref.shape[1]
    brick = size * rows_y
    chunks = nb // CHUNK
    rows = CHUNK * brick
    half = size // 2
    has_low, has_high = gy > 0, gy < n_gy - 1
    volume = 1.0 / (rows_y * n_gy * depth)

    barrier = pltpu.get_barrier_semaphore()
    for device in (left, right):
        pl.semaphore_signal(barrier, device_id={"gx": device}, device_id_type=pl.DeviceIdType.MESH)
    for off in range(1, n_gy):
        pl.semaphore_signal(
            barrier, device_id={"gy": lax.rem(gy + off, n_gy)}, device_id_type=pl.DeviceIdType.MESH
        )
    for j in range(own_slots):
        for a in range(nb):
            pack[j, a] = jnp.concatenate([kern_ref[j, a], wght_ref[j, a]], axis=1)
    pl.semaphore_wait(barrier, 2 + n_gy - 1)

    def x_copy(to_right, c):
        piece = pl.ds(pl.multiple_of(c * rows, rows), rows)
        group = 0 if to_right else 2
        return remote(
            x_ref.at[piece], raw.at[group, piece], x_send.at[group, c], x_recv.at[group, c],
            gx=right if to_right else left,
        )

    def start_x(c):
        x_copy(True, c).start()
        x_copy(False, c).start()

    loop(chunks, start_x)

    def k_copy(off):
        mine = pl.ds(gy * own_slots, own_slots)
        return remote(
            pack, packs.at[mine], k_send.at[off - 1], k_recv.at[off - 1], gy=lax.rem(gy + off, n_gy)
        )

    for off in range(1, n_gy):
        k_copy(off).start()
    own_copy = pltpu.make_async_copy(pack, packs.at[pl.ds(gy * own_slots, own_slots)], k_own)
    own_copy.start()

    def base_of(p):
        return pl.multiple_of(p * brick, brick)

    def spread(group, c, source):
        for i in range(CHUNK):
            b = c * CHUNK + i
            p = group * nb + b
            wide[pl.ds(base_of(p), brick), :] = source(b).astype(f32)
            for y in range(rows_y):
                row = wide[pl.ds(base_of(p) + y, size, stride=rows_y), :].astype(bf16)
                near_phi[p, :, y * depth : (y + 1) * depth] = row
                if y == 0:
                    edge_send[0, p] = row
                if y == rows_y - 1:
                    edge_send[1, p] = row

    def edge_copy(side, group, c):
        piece = pl.ds(group * nb + c * CHUNK, CHUNK)
        index = group * chunks + c
        return remote(
            edge_send.at[side, piece], edge_recv.at[1 - side, piece],
            e_send.at[side, index], e_recv.at[1 - side, index],
            gy=jnp.maximum(gy - 1, 0) if side == 0 else jnp.minimum(gy + 1, n_gy - 1),
        )

    def both_sides(action):
        pl.when(has_low)(lambda: action(0))
        pl.when(has_high)(lambda: action(1))

    def own_chunk(c):
        spread(1, c, lambda b: x_ref[pl.ds(pl.multiple_of(b * brick, brick), brick), :])
        both_sides(lambda side: edge_copy(side, 1, c).start())

    def far_chunk(group, c):
        piece = pl.ds(pl.multiple_of(c * rows, rows), rows)
        remote(
            x_ref.at[piece], raw.at[group, piece], x_send.at[group, c], x_recv.at[group, c], gx=right
        ).wait_recv()
        spread(group, c, lambda b: raw[group, pl.ds(pl.multiple_of(b * brick, brick), brick), :])
        both_sides(lambda side: edge_copy(side, group, c).start())

    def apply_chunk(group, c):
        pl.when(has_low)(lambda: edge_copy(1, group, c).wait_recv())
        pl.when(has_high)(lambda: edge_copy(0, group, c).wait_recv())
        for i in range(CHUNK):
            p = group * nb + c * CHUNK + i
            base = base_of(p)
            line = [edge_recv[0, p].astype(f32)]
            line += [wide[pl.ds(base + y, size, stride=rows_y), :] for y in range(rows_y)]
            line += [edge_recv[1, p].astype(f32)]
            for y in range(rows_y):
                center = line[y + 1]
                beside = (
                    line[y + 2] + line[y] + pltpu.roll(center, 1, 1) + pltpu.roll(center, depth - 1, 1)
                )
                applied = -0.5 * (beside - 4.0 * center) + pot_ref[y : y + 1, :] * center
                near_app[p, :, y * depth : (y + 1) * depth] = applied.astype(bf16)

    @pl.when(gy == 0)
    def _():
        edge_recv[0] = jnp.zeros(edge_recv.shape[1:], bf16)
        halo_recv[0] = jnp.zeros(halo_recv.shape[1:], bf16)

    @pl.when(gy == n_gy - 1)
    def _():
        edge_recv[1] = jnp.zeros(edge_recv.shape[1:], bf16)
        halo_recv[1] = jnp.zeros(halo_recv.shape[1:], bf16)

    first = 2 - 2 * lax.rem(gx, 2)
    second = 2 - first
    loop(chunks, own_chunk)
    loop(chunks, lambda c: far_chunk(first, c))
    loop(chunks, lambda c: apply_chunk(1, c))
    for off in range(1, n_gy):
        k_copy(off).wait_recv()
    own_copy.wait()
    loop(chunks, lambda c: far_chunk(second, c))
    loop(chunks, lambda c: apply_chunk(first, c))
    loop(chunks, lambda c: apply_chunk(second, c))

    def picks(a):
        start = nb * n_gx + nb - nb * gx
        found = [lax.rem(cols_ref[a, k] + start, nb * n_gx) for k in range(slots)]
        return [jnp.minimum(p, 3 * nb - 1) for p in found]

    def halo_copy(side, a):
        return remote(
            halo_send.at[side, a], halo_recv.at[1 - side, a], g_send.at[side, a], g_recv.at[1 - side, a],
            gy=jnp.maximum(gy - 1, 0) if side == 0 else jnp.minimum(gy + 1, n_gy - 1),
        )

    def gradient_of(a):
        where = picks(a)
        blocks = [packs[k, a] for k in range(slots)]
        mixing = jnp.concatenate(
            [b[:, :size] for b in blocks] + [-b[:, size:] for b in blocks], axis=1
        )
        source = jnp.concatenate([near_app[p] for p in where] + [near_phi[p] for p in where], axis=0)
        total = jnp.dot(mixing, source, preferred_element_type=f32)
        for y in range(rows_y):
            piece = total[:, y * depth : (y + 1) * depth]
            grad[a, y] = piece
            if y < SWEEPS:
                halo_send[0, a, y] = piece.astype(bf16)
            if y >= rows_y - SWEEPS:
                halo_send[1, a, y - rows_y + SWEEPS] = piece.astype(bf16)
        both_sides(lambda side: halo_copy(side, a).start())

    loop(nb, gradient_of)

    def part_of(a):
        source = jnp.concatenate([near_app[p] for p in picks(a)], axis=0)
        block = lax.dot_general(
            near_phi[nb + a], source, (((1,), (1,)), ((), ())), preferred_element_type=f32
        ) * volume
        for k in range(slots):
            one = block[:, k * size : (k + 1) * size]
            part[k, a] = jnp.concatenate([one[:half], one[half:]], axis=1)

    loop(nb, part_of)

    def part_copy(off):
        peer = lax.rem(gy + off, n_gy)
        return remote(
            part.at[pl.ds(peer * own_slots, own_slots)], part_recv.at[off - 1],
            h_send.at[off - 1], h_recv.at[off - 1], gy=peer,
        )

    for off in range(1, n_gy):
        part_copy(off).start()

    diag = 1.0 + 2.0 / kinetic_cut
    coef = 0.5 / kinetic_cut
    low, high = jnp.where(has_low, 1.0, 0.0).astype(f32), jnp.where(has_high, 1.0, 0.0).astype(f32)
    z_index = lax.broadcasted_iota(jnp.int32, (size, depth), 1)

    def finish(a):
        pl.when(has_low)(lambda: halo_copy(1, a).wait_recv())
        pl.when(has_high)(lambda: halo_copy(0, a).wait_recv())
        field = [halo_recv[0, a, i].astype(f32) for i in range(SWEEPS)]
        field += [grad[a, y] for y in range(rows_y)]
        field += [halo_recv[1, a, i].astype(f32) for i in range(SWEEPS)]
        field = [value * (1.0 / diag) for value in field]
        now = list(field)
        for sweep in range(1, SWEEPS + 1):
            later = list(now)
            for i in range(sweep, rows_y + 2 * SWEEPS - sweep):
                beside = now[i - 1] + now[i + 1]
                beside = beside + pltpu.roll(now[i], 1, 1) + pltpu.roll(now[i], depth - 1, 1)
                value = field[i] + (coef / diag) * beside
                if i < SWEEPS:
                    value = value * low
                if i >= rows_y + SWEEPS:
                    value = value * high
                later[i] = value
            now = later
        z_in = (z_index >= regs_ref[a, 2]) & (z_index < regs_ref[a, 3])
        base = base_of(nb + a)
        for y in range(rows_y):
            spot = gy * rows_y + y
            y_in = jnp.where((spot >= regs_ref[a, 0]) & (spot < regs_ref[a, 1]), step_length, 0.0)
            masked = jnp.where(z_in, now[SWEEPS + y] * y_in.astype(f32), 0.0)
            phi = wide[pl.ds(base + y, size, stride=rows_y), :]
            out_ref[pl.ds(pl.multiple_of(a * brick, brick) + y, size, stride=rows_y), :] = phi - masked

    loop(nb, finish)

    for off in range(1, n_gy):
        part_copy(off).wait_recv()
    for j in range(own_slots):
        for a in range(nb):
            total = part[gy * own_slots + j, a]
            for off in range(1, n_gy):
                total = total + part_recv[off - 1, j, a]
            ham_ref[j, a, :half, :] = total[:, :size]
            ham_ref[j, a, half:, :] = total[:, size:]

    def sent_x(c):
        x_copy(True, c).wait_send()
        x_copy(False, c).wait_send()

    loop(chunks, sent_x)
    for group in range(3):
        loop(chunks, lambda c: both_sides(lambda side: edge_copy(side, group, c).wait_send()))
    loop(nb, lambda a: both_sides(lambda side: halo_copy(side, a).wait_send()))
    for off in range(1, n_gy):
        k_copy(off).wait_send()
        part_copy(off).wait_send()


def local(n_gx, n_gy, support_funcs, potential, kernel, weighted, columns, regions):
    own_slots, nb, size = kernel.shape[:3]
    orbitals, rows_y, depth = support_funcs.shape
    slots = own_slots * n_gy
    flat = orbitals * rows_y
    chunks = nb // CHUNK
    vmem = pl.BlockSpec(memory_space=pltpu.VMEM)
    smem = pl.BlockSpec(memory_space=pltpu.SMEM)
    dma = pltpu.SemaphoreType.DMA
    new_support, hamiltonian = pl.pallas_call(
        functools.partial(kernel_body, n_gx, n_gy, rows_y),
        out_shape=(
            jax.ShapeDtypeStruct((flat, depth), f32),
            jax.ShapeDtypeStruct((own_slots, nb, size, size), f32),
        ),
        in_specs=[smem, smem, vmem, vmem, vmem, vmem],
        out_specs=(vmem, vmem),
        scratch_shapes=[
            pltpu.VMEM((3, flat, depth), bf16),
            pltpu.VMEM((3 * flat, depth), f32),
            pltpu.VMEM((3 * nb, size, rows_y * depth), bf16),
            pltpu.VMEM((3 * nb, size, rows_y * depth), bf16),
            pltpu.VMEM((2, 3 * nb, size, depth), bf16),
            pltpu.VMEM((2, 3 * nb, size, depth), bf16),
            pltpu.VMEM((own_slots, nb, size, 2 * size), bf16),
            pltpu.VMEM((slots, nb, size, 2 * size), bf16),
            pltpu.VMEM((nb, rows_y, size, depth), f32),
            pltpu.VMEM((2, nb, SWEEPS, size, depth), bf16),
            pltpu.VMEM((2, nb, SWEEPS, size, depth), bf16),
            pltpu.VMEM((slots, nb, size // 2, 2 * size), f32),
            pltpu.VMEM((n_gy - 1, own_slots, nb, size // 2, 2 * size), f32),
            dma((3, chunks)),
            dma((3, chunks)),
            dma((2, 3 * chunks)),
            dma((2, 3 * chunks)),
            dma((n_gy - 1,)),
            dma((n_gy - 1,)),
            dma(()),
            dma((2, nb)),
            dma((2, nb)),
            dma((n_gy - 1,)),
            dma((n_gy - 1,)),
        ],
        compiler_params=pltpu.CompilerParams(
            collective_id=0, has_side_effects=True, vmem_limit_bytes=40 * 1024 * 1024
        ),
    )(columns, regions, potential, support_funcs.reshape(flat, depth), kernel, weighted)
    return (new_support.reshape(orbitals, rows_y, depth), hamiltonian)


def solution(mesh):
    return jax.shard_map(
        functools.partial(local, mesh.shape["gx"], mesh.shape["gy"]),
        mesh=mesh,
        in_specs=(
            P("gx", "gy", None),
            P("gy", None),
            P("gy", "gx", None, None),
            P("gy", "gx", None, None),
            P("gx", None),
            P("gx", None),
        ),
        out_specs=(P("gx", "gy", None), P("gy", "gx", None, None)),
        check_vma=False,
    )
```

```python
import functools

import jax
import jax.numpy as jnp
from jax import lax
from jax.experimental import pallas as pl
from jax.experimental.pallas import tpu as pltpu
from jax.sharding import PartitionSpec as P

SWEEPS = 3
CHUNK = 2
kinetic_cut = 1.0
step_length = 0.5
f32 = jnp.float32
bf16 = jnp.bfloat16


def remote(src, dst, send, recv, **device):
    return pltpu.make_async_remote_copy(
        src_ref=src,
        dst_ref=dst,
        send_sem=send,
        recv_sem=recv,
        device_id=device,
        device_id_type=pl.DeviceIdType.MESH,
    )


def unrolled(count, body):
    for i in range(count):
        body(i)


def loop(count, body):
    def step(i, carry):
        body(i)
        return carry

    lax.fori_loop(0, count, step, 0)


def kernel_body(
    n_gx, n_gy, rows_y,
    cols_hbm, regs_hbm, pot_hbm, x_hbm, kern_hbm, wght_hbm,
    out_ref, ham_ref,
    cols_ref, regs_ref, pot_ref, x_ref, kern_ref, wght_ref, raw, wide, near_phi, near_app, edge_send, edge_recv, pack, packs,
    grad, halo_send, halo_recv, part, part_half, part_recv, half_recv, in_sem,
    x_send, x_recv, e_send, e_recv, k_send, k_recv, k_own, g_send, g_recv, h_send, h_recv, b_send, b_recv,
):
    gx, gy = lax.axis_index("gx"), lax.axis_index("gy")
    right, left = lax.rem(gx + 1, n_gx), lax.rem(gx + n_gx - 1, n_gx)
    own_slots, nb, size = kern_ref.shape[:3]
    slots = own_slots * n_gy
    depth = x_ref.shape[1]
    brick = size * rows_y
    chunks = nb // CHUNK
    rows = CHUNK * brick
    half = size // 2
    has_low, has_high = gy > 0, gy < n_gy - 1
    volume = 1.0 / (rows_y * n_gy * depth)

    pairs = (
        (x_hbm, x_ref), (kern_hbm, kern_ref), (wght_hbm, wght_ref),
        (pot_hbm, pot_ref), (cols_hbm, cols_ref), (regs_hbm, regs_ref),
    )
    loads = [pltpu.make_async_copy(src, dst, in_sem.at[i]) for i, (src, dst) in enumerate(pairs)]
    for load in loads:
        load.start()
    barrier = pltpu.get_barrier_semaphore()
    for device in (left, right):
        pl.semaphore_signal(barrier, device_id={"gx": device}, device_id_type=pl.DeviceIdType.MESH)
    for off in range(1, n_gy):
        pl.semaphore_signal(
            barrier, device_id={"gy": lax.rem(gy + off, n_gy)}, device_id_type=pl.DeviceIdType.MESH
        )
    loads[1].wait()
    loads[2].wait()
    for j in range(own_slots):
        for a in range(nb):
            pack[j, a] = jnp.concatenate([kern_ref[j, a], wght_ref[j, a]], axis=1)
    pl.semaphore_wait(barrier, 2 + n_gy - 1)

    def x_copy(to_right, c):
        piece = pl.ds(pl.multiple_of(c * rows, rows), rows)
        group = 0 if to_right else 2
        return remote(
            x_hbm.at[piece], raw.at[group, piece], x_send.at[group, c], x_recv.at[group, c],
            gx=right if to_right else left,
        )

    def start_x(c):
        x_copy(True, c).start()
        x_copy(False, c).start()

    loop(chunks, start_x)

    def k_copy(off):
        mine = pl.ds(gy * own_slots, own_slots)
        return remote(
            pack, packs.at[mine], k_send.at[off - 1], k_recv.at[off - 1], gy=lax.rem(gy + off, n_gy)
        )

    for off in range(1, n_gy):
        k_copy(off).start()
    own_copy = pltpu.make_async_copy(pack, packs.at[pl.ds(gy * own_slots, own_slots)], k_own)
    own_copy.start()

    def base_of(p):
        if isinstance(p, int):
            return p * brick
        return pl.multiple_of(p * brick, brick)

    def spread(group, c, source):
        for i in range(CHUNK):
            b = c * CHUNK + i
            p = group * nb + b
            wide[pl.ds(base_of(p), brick), :] = source(b).astype(f32)
            for y in range(rows_y):
                row = wide[pl.ds(base_of(p) + y, size, stride=rows_y), :].astype(bf16)
                near_phi[p, :, y * depth : (y + 1) * depth] = row
                if y == 0:
                    edge_send[0, p] = row
                if y == rows_y - 1:
                    edge_send[1, p] = row

    def edge_copy(side, group, c):
        piece = pl.ds(group * nb + c * CHUNK, CHUNK)
        index = group * chunks + c
        return remote(
            edge_send.at[side, piece], edge_recv.at[1 - side, piece],
            e_send.at[side, index], e_recv.at[1 - side, index],
            gy=jnp.maximum(gy - 1, 0) if side == 0 else jnp.minimum(gy + 1, n_gy - 1),
        )

    def both_sides(action):
        pl.when(has_low)(lambda: action(0))
        pl.when(has_high)(lambda: action(1))

    def own_chunk(c):
        spread(1, c, lambda b: x_ref[pl.ds(pl.multiple_of(b * brick, brick), brick), :])
        both_sides(lambda side: edge_copy(side, 1, c).start())

    def far_chunk(group, c):
        piece = pl.ds(pl.multiple_of(c * rows, rows), rows)
        remote(
            x_hbm.at[piece], raw.at[group, piece], x_send.at[group, c], x_recv.at[group, c], gx=right
        ).wait_recv()
        spread(group, c, lambda b: raw[group, pl.ds(pl.multiple_of(b * brick, brick), brick), :])
        both_sides(lambda side: edge_copy(side, group, c).start())

    def apply_chunk(group, c):
        pl.when(has_low)(lambda: edge_copy(1, group, c).wait_recv())
        pl.when(has_high)(lambda: edge_copy(0, group, c).wait_recv())
        for i in range(CHUNK):
            p = group * nb + c * CHUNK + i
            base = base_of(p)
            line = [edge_recv[0, p].astype(f32)]
            line += [wide[pl.ds(base + y, size, stride=rows_y), :] for y in range(rows_y)]
            line += [edge_recv[1, p].astype(f32)]
            for y in range(rows_y):
                center = line[y + 1]
                beside = (
                    line[y + 2] + line[y] + pltpu.roll(center, 1, 1) + pltpu.roll(center, depth - 1, 1)
                )
                applied = -0.5 * (beside - 4.0 * center) + pot_ref[y : y + 1, :] * center
                near_app[p, :, y * depth : (y + 1) * depth] = applied.astype(bf16)

    @pl.when(gy == 0)
    def _():
        edge_recv[0] = jnp.zeros(edge_recv.shape[1:], bf16)
        halo_recv[0] = jnp.zeros(halo_recv.shape[1:], bf16)

    @pl.when(gy == n_gy - 1)
    def _():
        edge_recv[1] = jnp.zeros(edge_recv.shape[1:], bf16)
        halo_recv[1] = jnp.zeros(halo_recv.shape[1:], bf16)

    first = 2 - 2 * lax.rem(gx, 2)
    second = 2 - first
    loads[0].wait()
    loop(chunks, own_chunk)
    for load in loads[3:]:
        load.wait()
    loop(chunks, lambda c: far_chunk(first, c))
    loop(chunks, lambda c: apply_chunk(1, c))
    for off in range(1, n_gy):
        k_copy(off).wait_recv()
    own_copy.wait()
    loop(chunks, lambda c: far_chunk(second, c))
    loop(chunks, lambda c: apply_chunk(first, c))
    loop(chunks, lambda c: apply_chunk(second, c))

    def picks(a):
        start = nb * n_gx + nb - nb * gx
        found = [lax.rem(cols_ref[k, a] + start, nb * n_gx) for k in range(slots)]
        return [jnp.minimum(p, 3 * nb - 1) for p in found]

    def halo_copy(side, a):
        return remote(
            halo_send.at[side, a], halo_recv.at[1 - side, a], g_send.at[side, a], g_recv.at[1 - side, a],
            gy=jnp.maximum(gy - 1, 0) if side == 0 else jnp.minimum(gy + 1, n_gy - 1),
        )

    def gradient_of(a):
        where = picks(a)
        blocks = [packs[k, a] for k in range(slots)]
        mixing = jnp.concatenate(
            [b[:, :size] for b in blocks] + [-b[:, size:] for b in blocks], axis=1
        )
        source = jnp.concatenate([near_app[p] for p in where] + [near_phi[p] for p in where], axis=0)
        total = jnp.dot(mixing, source, preferred_element_type=f32)
        for y in range(rows_y):
            piece = total[:, y * depth : (y + 1) * depth]
            grad[a, y] = piece
            if y < SWEEPS:
                halo_send[0, a, y] = piece.astype(bf16)
            if y >= rows_y - SWEEPS:
                halo_send[1, a, y - rows_y + SWEEPS] = piece.astype(bf16)
        both_sides(lambda side: halo_copy(side, a).start())

    unrolled(nb, gradient_of)

    def part_of(a):
        source = jnp.concatenate([near_app[p] for p in picks(a)], axis=0)
        block = lax.dot_general(
            near_phi[nb + a], source, (((1,), (1,)), ((), ())), preferred_element_type=f32
        ) * volume
        for k in range(slots):
            one = block[:, k * size : (k + 1) * size]
            one = jnp.concatenate([one[:half], one[half:]], axis=1)
            part[k, a] = one
            part_half[k, a] = one.astype(bf16)

    unrolled(nb, part_of)

    def part_copy(off, wide_type):
        peer = lax.rem(gy + off, n_gy)
        source, target = (part, part_recv) if wide_type else (part_half, half_recv)
        send, recv = (h_send, h_recv) if wide_type else (b_send, b_recv)
        return remote(
            source.at[pl.ds(peer * own_slots, own_slots)], target.at[off - 1],
            send.at[off - 1], recv.at[off - 1], gy=peer,
        )

    def by_distance(off, other, action):
        apart = jnp.abs(other - gy)
        pl.when(apart == 1)(lambda: action(off, True))
        pl.when(apart > 1)(lambda: action(off, False))

    for off in range(1, n_gy):
        by_distance(off, lax.rem(gy + off, n_gy), lambda o, w: part_copy(o, w).start())

    diag = 1.0 + 2.0 / kinetic_cut
    coef = 0.5 / kinetic_cut
    low, high = jnp.where(has_low, 1.0, 0.0).astype(f32), jnp.where(has_high, 1.0, 0.0).astype(f32)
    z_index = lax.broadcasted_iota(jnp.int32, (size, depth), 1)

    def finish(a):
        pl.when(has_low)(lambda: halo_copy(1, a).wait_recv())
        pl.when(has_high)(lambda: halo_copy(0, a).wait_recv())
        field = [halo_recv[0, a, i].astype(f32) for i in range(SWEEPS)]
        field += [grad[a, y] for y in range(rows_y)]
        field += [halo_recv[1, a, i].astype(f32) for i in range(SWEEPS)]
        field = [value * (1.0 / diag) for value in field]
        now = list(field)
        for sweep in range(1, SWEEPS + 1):
            later = list(now)
            for i in range(sweep, rows_y + 2 * SWEEPS - sweep):
                beside = now[i - 1] + now[i + 1]
                beside = beside + pltpu.roll(now[i], 1, 1) + pltpu.roll(now[i], depth - 1, 1)
                value = field[i] + (coef / diag) * beside
                if i < SWEEPS:
                    value = value * low
                if i >= rows_y + SWEEPS:
                    value = value * high
                later[i] = value
            now = later
        z_in = (z_index >= regs_ref[2, a]) & (z_index < regs_ref[3, a])
        base = base_of(nb + a)
        for y in range(rows_y):
            spot = gy * rows_y + y
            y_in = jnp.where((spot >= regs_ref[0, a]) & (spot < regs_ref[1, a]), step_length, 0.0)
            masked = jnp.where(z_in, now[SWEEPS + y] * y_in.astype(f32), 0.0)
            phi = wide[pl.ds(base + y, size, stride=rows_y), :]
            out_ref[pl.ds(a * brick + y, size, stride=rows_y), :] = phi - masked

    unrolled(nb, finish)

    mine = pl.ds(gy * own_slots, own_slots)

    def take(off, wide_type):
        part_copy(off, wide_type).wait_recv()
        part[mine] = part[mine] + (part_recv if wide_type else half_recv)[off - 1].astype(f32)

    for off in range(1, n_gy):
        by_distance(off, lax.rem(gy + n_gy - off, n_gy), take)
    for j in range(own_slots):
        for a in range(nb):
            total = part[gy * own_slots + j, a]
            ham_ref[j, a, :half, :] = total[:, :size]
            ham_ref[j, a, half:, :] = total[:, size:]

    def sent_x(c):
        x_copy(True, c).wait_send()
        x_copy(False, c).wait_send()

    loop(chunks, sent_x)
    for group in range(3):
        loop(chunks, lambda c: both_sides(lambda side: edge_copy(side, group, c).wait_send()))
    loop(nb, lambda a: both_sides(lambda side: halo_copy(side, a).wait_send()))
    for off in range(1, n_gy):
        k_copy(off).wait_send()
        by_distance(off, lax.rem(gy + off, n_gy), lambda o, w: part_copy(o, w).wait_send())


def store_body(support_ref, ham_ref, support_out, ham_out, sem):
    copies = [
        pltpu.make_async_copy(support_ref, support_out, sem.at[0]),
        pltpu.make_async_copy(ham_ref, ham_out, sem.at[1]),
    ]
    for copy in copies:
        copy.start()
    for copy in copies:
        copy.wait()


def local(n_gx, n_gy, support_funcs, potential, kernel, weighted, columns, regions):
    own_slots, nb, size = kernel.shape[:3]
    orbitals, rows_y, depth = support_funcs.shape
    slots = own_slots * n_gy
    flat = orbitals * rows_y
    chunks = nb // CHUNK
    vmem = pl.BlockSpec(memory_space=pltpu.VMEM)
    dma = pltpu.SemaphoreType.DMA
    operands = (
        columns.T, regions.T, potential, support_funcs.reshape(flat, depth), kernel, weighted
    )
    new_support, hamiltonian = pl.pallas_call(
        functools.partial(kernel_body, n_gx, n_gy, rows_y),
        out_shape=(
            jax.ShapeDtypeStruct((flat, depth), f32),
            jax.ShapeDtypeStruct((own_slots, nb, size, size), f32),
        ),
        in_specs=[pl.BlockSpec(memory_space=pltpu.HBM)] * 6,
        out_specs=(vmem, vmem),
        scratch_shapes=[
            pltpu.SMEM((slots, nb), jnp.int32),
            pltpu.SMEM((4, nb), jnp.int32),
            pltpu.VMEM((rows_y, depth), f32),
            pltpu.VMEM((flat, depth), bf16),
            pltpu.VMEM(kernel.shape, bf16),
            pltpu.VMEM(kernel.shape, bf16),
            pltpu.VMEM((3, flat, depth), bf16),
            pltpu.VMEM((3 * flat, depth), f32),
            pltpu.VMEM((3 * nb, size, rows_y * depth), bf16),
            pltpu.VMEM((3 * nb, size, rows_y * depth), bf16),
            pltpu.VMEM((2, 3 * nb, size, depth), bf16),
            pltpu.VMEM((2, 3 * nb, size, depth), bf16),
            pltpu.VMEM((own_slots, nb, size, 2 * size), bf16),
            pltpu.VMEM((slots, nb, size, 2 * size), bf16),
            pltpu.VMEM((nb, rows_y, size, depth), f32),
            pltpu.VMEM((2, nb, SWEEPS, size, depth), bf16),
            pltpu.VMEM((2, nb, SWEEPS, size, depth), bf16),
            pltpu.VMEM((slots, nb, size // 2, 2 * size), f32),
            pltpu.VMEM((slots, nb, size // 2, 2 * size), bf16),
            pltpu.VMEM((n_gy - 1, own_slots, nb, size // 2, 2 * size), f32),
            pltpu.VMEM((n_gy - 1, own_slots, nb, size // 2, 2 * size), bf16),
            dma((6,)),
            dma((3, chunks)),
            dma((3, chunks)),
            dma((2, 3 * chunks)),
            dma((2, 3 * chunks)),
            dma((n_gy - 1,)),
            dma((n_gy - 1,)),
            dma(()),
            dma((2, nb)),
            dma((2, nb)),
            dma((n_gy - 1,)),
            dma((n_gy - 1,)),
            dma((n_gy - 1,)),
            dma((n_gy - 1,)),
        ],
        compiler_params=pltpu.CompilerParams(
            collective_id=0, has_side_effects=True, vmem_limit_bytes=40 * 1024 * 1024
        ),
    )(*[pltpu.with_memory_space_constraint(v, pltpu.HBM) for v in operands])
    hbm = pl.BlockSpec(memory_space=pltpu.HBM)
    new_support, hamiltonian = pl.pallas_call(
        store_body,
        out_shape=(
            jax.ShapeDtypeStruct(new_support.shape, f32),
            jax.ShapeDtypeStruct(hamiltonian.shape, f32),
        ),
        in_specs=[vmem, vmem],
        out_specs=(hbm, hbm),
        scratch_shapes=[dma((2,))],
    )(new_support, hamiltonian)
    return (new_support.reshape(orbitals, rows_y, depth), hamiltonian)


def solution(mesh):
    return jax.shard_map(
        functools.partial(local, mesh.shape["gx"], mesh.shape["gy"]),
        mesh=mesh,
        in_specs=(
            P("gx", "gy", None),
            P("gy", None),
            P("gy", "gx", None, None),
            P("gy", "gx", None, None),
            P("gx", None),
            P("gx", None),
        ),
        out_specs=(P("gx", "gy", None), P("gy", "gx", None, None)),
        check_vma=False,
    )
```

```python
import functools

import jax
import jax.numpy as jnp
from jax import lax
from jax.experimental import pallas as pl
from jax.experimental.pallas import tpu as pltpu
from jax.sharding import PartitionSpec as P

SWEEPS = 3
CHUNK = 2
kinetic_cut = 1.0
step_length = 0.5
f32 = jnp.float32
bf16 = jnp.bfloat16


def remote(src, dst, send, recv, **device):
    return pltpu.make_async_remote_copy(
        src_ref=src,
        dst_ref=dst,
        send_sem=send,
        recv_sem=recv,
        device_id=device,
        device_id_type=pl.DeviceIdType.MESH,
    )


def unrolled(count, body):
    for i in range(count):
        body(i)


def loop(count, body):
    def step(i, carry):
        body(i)
        return carry

    lax.fori_loop(0, count, step, 0)


def kernel_body(
    n_gx, n_gy, rows_y,
    cols_hbm, regs_hbm, pot_hbm, x_hbm, kern_hbm, wght_hbm,
    out_ref, ham_ref,
    cols_ref, regs_ref, pot_ref, x_ref, kern_ref, wght_ref, raw, wide, near_phi, near_app, edge_send, edge_recv, pack, packs,
    grad, halo_send, halo_recv, part, part_half, part_recv, half_recv, in_sem,
    x_send, x_recv, e_send, e_recv, k_send, k_recv, k_own, g_send, g_recv, h_send, h_recv, b_send, b_recv,
):
    gx, gy = lax.axis_index("gx"), lax.axis_index("gy")
    right, left = lax.rem(gx + 1, n_gx), lax.rem(gx + n_gx - 1, n_gx)
    own_slots, nb, size = kern_ref.shape[:3]
    slots = own_slots * n_gy
    depth = x_ref.shape[1]
    brick = size * rows_y
    chunks = nb // CHUNK
    rows = CHUNK * brick
    half = size // 2
    has_low, has_high = gy > 0, gy < n_gy - 1
    volume = 1.0 / (rows_y * n_gy * depth)

    pairs = (
        (x_hbm, x_ref), (kern_hbm, kern_ref), (wght_hbm, wght_ref),
        (pot_hbm, pot_ref), (cols_hbm, cols_ref), (regs_hbm, regs_ref),
    )
    loads = [pltpu.make_async_copy(src, dst, in_sem.at[i]) for i, (src, dst) in enumerate(pairs)]
    for load in loads:
        load.start()
    barrier = pltpu.get_barrier_semaphore()
    for device in (left, right):
        pl.semaphore_signal(barrier, device_id={"gx": device}, device_id_type=pl.DeviceIdType.MESH)
    for off in range(1, n_gy):
        pl.semaphore_signal(
            barrier, device_id={"gy": lax.rem(gy + off, n_gy)}, device_id_type=pl.DeviceIdType.MESH
        )
    loads[1].wait()
    loads[2].wait()
    for j in range(own_slots):
        for a in range(nb):
            pack[j, a] = jnp.concatenate([kern_ref[j, a], wght_ref[j, a]], axis=1)
    pl.semaphore_wait(barrier, 2 + n_gy - 1)

    def x_copy(to_right, c):
        piece = pl.ds(pl.multiple_of(c * rows, rows), rows)
        group = 0 if to_right else 2
        return remote(
            x_hbm.at[piece], raw.at[group, piece], x_send.at[group, c], x_recv.at[group, c],
            gx=right if to_right else left,
        )

    def start_x(c):
        x_copy(True, c).start()
        x_copy(False, c).start()

    unrolled(chunks, start_x)

    def k_copy(off):
        mine = pl.ds(gy * own_slots, own_slots)
        return remote(
            pack, packs.at[mine], k_send.at[off - 1], k_recv.at[off - 1], gy=lax.rem(gy + off, n_gy)
        )

    for off in range(1, n_gy):
        k_copy(off).start()
    own_copy = pltpu.make_async_copy(pack, packs.at[pl.ds(gy * own_slots, own_slots)], k_own)
    own_copy.start()

    def base_of(p):
        if isinstance(p, int):
            return p * brick
        return pl.multiple_of(p * brick, brick)

    def spread(group, c, source):
        for i in range(CHUNK):
            b = c * CHUNK + i
            p = group * nb + b
            wide[pl.ds(base_of(p), brick), :] = source(b).astype(f32)
            for y in range(rows_y):
                row = wide[pl.ds(base_of(p) + y, size, stride=rows_y), :].astype(bf16)
                near_phi[p, :, y * depth : (y + 1) * depth] = row
                if y == 0:
                    edge_send[0, p] = row
                if y == rows_y - 1:
                    edge_send[1, p] = row

    def edge_copy(side, group, c):
        piece = pl.ds(group * nb + c * CHUNK, CHUNK)
        index = group * chunks + c
        return remote(
            edge_send.at[side, piece], edge_recv.at[1 - side, piece],
            e_send.at[side, index], e_recv.at[1 - side, index],
            gy=jnp.maximum(gy - 1, 0) if side == 0 else jnp.minimum(gy + 1, n_gy - 1),
        )

    def both_sides(action):
        pl.when(has_low)(lambda: action(0))
        pl.when(has_high)(lambda: action(1))

    def own_chunk(c):
        spread(1, c, lambda b: x_ref[pl.ds(pl.multiple_of(b * brick, brick), brick), :])
        both_sides(lambda side: edge_copy(side, 1, c).start())

    def far_chunk(group, c):
        piece = pl.ds(pl.multiple_of(c * rows, rows), rows)
        remote(
            x_hbm.at[piece], raw.at[group, piece], x_send.at[group, c], x_recv.at[group, c], gx=right
        ).wait_recv()
        spread(group, c, lambda b: raw[group, pl.ds(pl.multiple_of(b * brick, brick), brick), :])
        both_sides(lambda side: edge_copy(side, group, c).start())

    def apply_chunk(group, c):
        pl.when(has_low)(lambda: edge_copy(1, group, c).wait_recv())
        pl.when(has_high)(lambda: edge_copy(0, group, c).wait_recv())
        for i in range(CHUNK):
            p = group * nb + c * CHUNK + i
            line = [edge_recv[0, p].astype(f32)]
            line += [
                near_phi[p, :, y * depth : (y + 1) * depth].astype(f32) for y in range(rows_y)
            ]
            line += [edge_recv[1, p].astype(f32)]
            for y in range(rows_y):
                center = line[y + 1]
                beside = (
                    line[y + 2] + line[y] + pltpu.roll(center, 1, 1) + pltpu.roll(center, depth - 1, 1)
                )
                applied = -0.5 * (beside - 4.0 * center) + pot_ref[y : y + 1, :] * center
                near_app[p, :, y * depth : (y + 1) * depth] = applied.astype(bf16)

    @pl.when(gy == 0)
    def _():
        edge_recv[0] = jnp.zeros(edge_recv.shape[1:], bf16)
        halo_recv[0] = jnp.zeros(halo_recv.shape[1:], bf16)

    @pl.when(gy == n_gy - 1)
    def _():
        edge_recv[1] = jnp.zeros(edge_recv.shape[1:], bf16)
        halo_recv[1] = jnp.zeros(halo_recv.shape[1:], bf16)

    first = 2 - 2 * lax.rem(gx, 2)
    second = 2 - first
    loads[0].wait()
    unrolled(chunks, own_chunk)
    for load in loads[3:]:
        load.wait()
    unrolled(chunks, lambda c: far_chunk(first, c))
    unrolled(chunks, lambda c: apply_chunk(1, c))
    for off in range(1, n_gy):
        k_copy(off).wait_recv()
    own_copy.wait()

    def interleaved(c):
        far_chunk(second, c)
        apply_chunk(first, c)

    unrolled(chunks, interleaved)
    unrolled(chunks, lambda c: apply_chunk(second, c))

    def picks(a):
        start = nb * n_gx + nb - nb * gx
        found = [lax.rem(cols_ref[k, a] + start, nb * n_gx) for k in range(slots)]
        return [jnp.minimum(p, 3 * nb - 1) for p in found]

    def halo_copy(side, a):
        return remote(
            halo_send.at[side, a], halo_recv.at[1 - side, a], g_send.at[side, a], g_recv.at[1 - side, a],
            gy=jnp.maximum(gy - 1, 0) if side == 0 else jnp.minimum(gy + 1, n_gy - 1),
        )

    def gradient_of(a):
        where = picks(a)
        blocks = [packs[k, a] for k in range(slots)]
        mixing = jnp.concatenate(
            [b[:, :size] for b in blocks] + [-b[:, size:] for b in blocks], axis=1
        )
        source = jnp.concatenate([near_app[p] for p in where] + [near_phi[p] for p in where], axis=0)
        total = jnp.dot(mixing, source, preferred_element_type=f32)
        for y in range(rows_y):
            piece = total[:, y * depth : (y + 1) * depth]
            grad[a, y] = piece
            if y < SWEEPS:
                halo_send[0, a, y] = piece.astype(bf16)
            if y >= rows_y - SWEEPS:
                halo_send[1, a, y - rows_y + SWEEPS] = piece.astype(bf16)
        both_sides(lambda side: halo_copy(side, a).start())

    unrolled(nb, gradient_of)

    def part_of(a):
        source = jnp.concatenate([near_app[p] for p in picks(a)], axis=0)
        block = lax.dot_general(
            near_phi[nb + a], source, (((1,), (1,)), ((), ())), preferred_element_type=f32
        ) * volume
        for k in range(slots):
            one = block[:, k * size : (k + 1) * size]
            one = jnp.concatenate([one[:half], one[half:]], axis=1)
            part[k, a] = one
            part_half[k, a] = one.astype(bf16)

    unrolled(nb, part_of)

    def part_copy(off, wide_type):
        peer = lax.rem(gy + off, n_gy)
        source, target = (part, part_recv) if wide_type else (part_half, half_recv)
        send, recv = (h_send, h_recv) if wide_type else (b_send, b_recv)
        return remote(
            source.at[pl.ds(peer * own_slots, own_slots)], target.at[off - 1],
            send.at[off - 1], recv.at[off - 1], gy=peer,
        )

    def by_distance(off, other, action):
        apart = jnp.abs(other - gy)
        pl.when(apart == 1)(lambda: action(off, True))
        pl.when(apart > 1)(lambda: action(off, False))

    for off in range(1, n_gy):
        by_distance(off, lax.rem(gy + off, n_gy), lambda o, w: part_copy(o, w).start())

    diag = 1.0 + 2.0 / kinetic_cut
    coef = 0.5 / kinetic_cut
    low, high = jnp.where(has_low, 1.0, 0.0).astype(f32), jnp.where(has_high, 1.0, 0.0).astype(f32)
    z_index = lax.broadcasted_iota(jnp.int32, (size, depth), 1)

    def finish(a):
        pl.when(has_low)(lambda: halo_copy(1, a).wait_recv())
        pl.when(has_high)(lambda: halo_copy(0, a).wait_recv())
        field = [halo_recv[0, a, i].astype(f32) for i in range(SWEEPS)]
        field += [grad[a, y] for y in range(rows_y)]
        field += [halo_recv[1, a, i].astype(f32) for i in range(SWEEPS)]
        field = [value * (1.0 / diag) for value in field]
        now = list(field)
        for sweep in range(1, SWEEPS + 1):
            later = list(now)
            for i in range(sweep, rows_y + 2 * SWEEPS - sweep):
                beside = now[i - 1] + now[i + 1]
                beside = beside + pltpu.roll(now[i], 1, 1) + pltpu.roll(now[i], depth - 1, 1)
                value = field[i] + (coef / diag) * beside
                if i < SWEEPS:
                    value = value * low
                if i >= rows_y + SWEEPS:
                    value = value * high
                later[i] = value
            now = later
        z_in = (z_index >= regs_ref[2, a]) & (z_index < regs_ref[3, a])
        for y in range(rows_y):
            spot = gy * rows_y + y
            y_in = jnp.where((spot >= regs_ref[0, a]) & (spot < regs_ref[1, a]), step_length, 0.0)
            masked = jnp.where(z_in, now[SWEEPS + y] * y_in.astype(f32), 0.0)
            phi = near_phi[nb + a, :, y * depth : (y + 1) * depth].astype(f32)
            out_ref[pl.ds(a * brick + y, size, stride=rows_y), :] = phi - masked

    unrolled(nb, finish)

    mine = pl.ds(gy * own_slots, own_slots)

    def take(off, wide_type):
        part_copy(off, wide_type).wait_recv()
        part[mine] = part[mine] + (part_recv if wide_type else half_recv)[off - 1].astype(f32)

    for off in range(1, n_gy):
        by_distance(off, lax.rem(gy + n_gy - off, n_gy), take)
    for j in range(own_slots):
        for a in range(nb):
            total = part[gy * own_slots + j, a]
            ham_ref[j, a, :half, :] = total[:, :size]
            ham_ref[j, a, half:, :] = total[:, size:]

    def sent_x(c):
        x_copy(True, c).wait_send()
        x_copy(False, c).wait_send()

    loop(chunks, sent_x)
    for group in range(3):
        loop(chunks, lambda c: both_sides(lambda side: edge_copy(side, group, c).wait_send()))
    loop(nb, lambda a: both_sides(lambda side: halo_copy(side, a).wait_send()))
    for off in range(1, n_gy):
        k_copy(off).wait_send()
        by_distance(off, lax.rem(gy + off, n_gy), lambda o, w: part_copy(o, w).wait_send())


def store_body(support_ref, ham_ref, support_out, ham_out, sem):
    copies = [
        pltpu.make_async_copy(support_ref, support_out, sem.at[0]),
        pltpu.make_async_copy(ham_ref, ham_out, sem.at[1]),
    ]
    for copy in copies:
        copy.start()
    for copy in copies:
        copy.wait()


def local(n_gx, n_gy, support_funcs, potential, kernel, weighted, columns, regions):
    own_slots, nb, size = kernel.shape[:3]
    orbitals, rows_y, depth = support_funcs.shape
    slots = own_slots * n_gy
    flat = orbitals * rows_y
    chunks = nb // CHUNK
    vmem = pl.BlockSpec(memory_space=pltpu.VMEM)
    dma = pltpu.SemaphoreType.DMA
    operands = (
        columns.T, regions.T, potential, support_funcs.reshape(flat, depth), kernel, weighted
    )
    new_support, hamiltonian = pl.pallas_call(
        functools.partial(kernel_body, n_gx, n_gy, rows_y),
        out_shape=(
            jax.ShapeDtypeStruct((flat, depth), f32),
            jax.ShapeDtypeStruct((own_slots, nb, size, size), f32),
        ),
        in_specs=[pl.BlockSpec(memory_space=pltpu.HBM)] * 6,
        out_specs=(vmem, vmem),
        scratch_shapes=[
            pltpu.SMEM((slots, nb), jnp.int32),
            pltpu.SMEM((4, nb), jnp.int32),
            pltpu.VMEM((rows_y, depth), f32),
            pltpu.VMEM((flat, depth), bf16),
            pltpu.VMEM(kernel.shape, bf16),
            pltpu.VMEM(kernel.shape, bf16),
            pltpu.VMEM((3, flat, depth), bf16),
            pltpu.VMEM((3 * flat, depth), f32),
            pltpu.VMEM((3 * nb, size, rows_y * depth), bf16),
            pltpu.VMEM((3 * nb, size, rows_y * depth), bf16),
            pltpu.VMEM((2, 3 * nb, size, depth), bf16),
            pltpu.VMEM((2, 3 * nb, size, depth), bf16),
            pltpu.VMEM((own_slots, nb, size, 2 * size), bf16),
            pltpu.VMEM((slots, nb, size, 2 * size), bf16),
            pltpu.VMEM((nb, rows_y, size, depth), f32),
            pltpu.VMEM((2, nb, SWEEPS, size, depth), bf16),
            pltpu.VMEM((2, nb, SWEEPS, size, depth), bf16),
            pltpu.VMEM((slots, nb, size // 2, 2 * size), f32),
            pltpu.VMEM((slots, nb, size // 2, 2 * size), bf16),
            pltpu.VMEM((n_gy - 1, own_slots, nb, size // 2, 2 * size), f32),
            pltpu.VMEM((n_gy - 1, own_slots, nb, size // 2, 2 * size), bf16),
            dma((6,)),
            dma((3, chunks)),
            dma((3, chunks)),
            dma((2, 3 * chunks)),
            dma((2, 3 * chunks)),
            dma((n_gy - 1,)),
            dma((n_gy - 1,)),
            dma(()),
            dma((2, nb)),
            dma((2, nb)),
            dma((n_gy - 1,)),
            dma((n_gy - 1,)),
            dma((n_gy - 1,)),
            dma((n_gy - 1,)),
        ],
        compiler_params=pltpu.CompilerParams(
            collective_id=0, has_side_effects=True, vmem_limit_bytes=40 * 1024 * 1024
        ),
    )(*[pltpu.with_memory_space_constraint(v, pltpu.HBM) for v in operands])
    hbm = pl.BlockSpec(memory_space=pltpu.HBM)
    new_support, hamiltonian = pl.pallas_call(
        store_body,
        out_shape=(
            jax.ShapeDtypeStruct(new_support.shape, f32),
            jax.ShapeDtypeStruct(hamiltonian.shape, f32),
        ),
        in_specs=[vmem, vmem],
        out_specs=(hbm, hbm),
        scratch_shapes=[dma((2,))],
        compiler_params=pltpu.CompilerParams(vmem_limit_bytes=8 * 1024 * 1024),
    )(new_support, hamiltonian)
    return (new_support.reshape(orbitals, rows_y, depth), hamiltonian)


def solution(mesh):
    return jax.shard_map(
        functools.partial(local, mesh.shape["gx"], mesh.shape["gy"]),
        mesh=mesh,
        in_specs=(
            P("gx", "gy", None),
            P("gy", None),
            P("gy", "gx", None, None),
            P("gy", "gx", None, None),
            P("gx", None),
            P("gx", None),
        ),
        out_specs=(P("gx", "gy", None), P("gy", "gx", None, None)),
        check_vma=False,
    )
```

```python
import functools

import jax
import jax.numpy as jnp
from jax import lax
from jax.experimental import pallas as pl
from jax.experimental.pallas import tpu as pltpu
from jax.sharding import PartitionSpec as P

SWEEPS = 3
CHUNK = 2
kinetic_cut = 1.0
step_length = 0.5
f32 = jnp.float32
bf16 = jnp.bfloat16


def remote(src, dst, send, recv, **device):
    return pltpu.make_async_remote_copy(
        src_ref=src,
        dst_ref=dst,
        send_sem=send,
        recv_sem=recv,
        device_id=device,
        device_id_type=pl.DeviceIdType.MESH,
    )


def unrolled(count, body):
    for i in range(count):
        body(i)


def loop(count, body):
    def step(i, carry):
        body(i)
        return carry

    lax.fori_loop(0, count, step, 0)


def kernel_body(
    n_gx, n_gy, rows_y,
    cols_hbm, regs_hbm, pot_hbm, x_hbm, kern_hbm, wght_hbm,
    out_ref, ham_ref,
    cols_ref, regs_ref, pot_ref, x_ref, kern_ref, wght_ref, raw, wide, near_phi, near_app, edge_send, edge_recv, pack, packs,
    grad, halo_send, halo_recv, part, part_half, part_recv, half_recv, in_sem,
    x_send, x_recv, e_send, e_recv, k_send, k_recv, k_own, g_send, g_recv, h_send, h_recv, b_send, b_recv,
):
    gx, gy = lax.axis_index("gx"), lax.axis_index("gy")
    right, left = lax.rem(gx + 1, n_gx), lax.rem(gx + n_gx - 1, n_gx)
    own_slots, nb, size = kern_ref.shape[:3]
    slots = own_slots * n_gy
    depth = x_ref.shape[1]
    brick = size * rows_y
    chunks = nb // CHUNK
    rows = CHUNK * brick
    half = size // 2
    has_low, has_high = gy > 0, gy < n_gy - 1
    volume = 1.0 / (rows_y * n_gy * depth)

    pairs = (
        (x_hbm, x_ref), (kern_hbm, kern_ref), (wght_hbm, wght_ref),
        (pot_hbm, pot_ref), (cols_hbm, cols_ref), (regs_hbm, regs_ref),
    )
    loads = [pltpu.make_async_copy(src, dst, in_sem.at[i]) for i, (src, dst) in enumerate(pairs)]
    for load in loads:
        load.start()
    barrier = pltpu.get_barrier_semaphore()
    for device in (left, right):
        pl.semaphore_signal(barrier, device_id={"gx": device}, device_id_type=pl.DeviceIdType.MESH)
    for off in range(1, n_gy):
        pl.semaphore_signal(
            barrier, device_id={"gy": lax.rem(gy + off, n_gy)}, device_id_type=pl.DeviceIdType.MESH
        )
    loads[1].wait()
    loads[2].wait()
    for j in range(own_slots):
        for a in range(nb):
            pack[j, a] = jnp.concatenate([kern_ref[j, a], wght_ref[j, a]], axis=1)
    pl.semaphore_wait(barrier, 2 + n_gy - 1)

    def x_copy(to_right, c):
        piece = pl.ds(pl.multiple_of(c * rows, rows), rows)
        group = 0 if to_right else 2
        return remote(
            x_hbm.at[piece], raw.at[group, piece], x_send.at[group, c], x_recv.at[group, c],
            gx=right if to_right else left,
        )

    def start_x(c):
        x_copy(True, c).start()
        x_copy(False, c).start()

    unrolled(chunks, start_x)

    def k_copy(up, d):
        origin = gy - (d - 1) if up else gy + (d - 1)
        place = pl.ds(jnp.clip(origin, 0, n_gy - 1) * own_slots, own_slots)
        side = 0 if up else 1
        return remote(
            pack if d == 1 else packs.at[place], packs.at[place],
            k_send.at[side, d - 1], k_recv.at[side, d - 1],
            gy=jnp.minimum(gy + 1, n_gy - 1) if up else jnp.maximum(gy - 1, 0),
        )

    def k_sends(d, action):
        pl.when((gy - (d - 1) >= 0) & has_high)(lambda: action(k_copy(True, d)))
        pl.when((gy + (d - 1) < n_gy) & has_low)(lambda: action(k_copy(False, d)))

    def k_arrived(d):
        pl.when(gy - d >= 0)(lambda: k_copy(True, d).wait_recv())
        pl.when(gy + d < n_gy)(lambda: k_copy(False, d).wait_recv())

    def k_relay(d):
        k_arrived(d - 1)
        k_sends(d, lambda copy: copy.start())

    k_sends(1, lambda copy: copy.start())
    own_copy = pltpu.make_async_copy(pack, packs.at[pl.ds(gy * own_slots, own_slots)], k_own)
    own_copy.start()

    def base_of(p):
        if isinstance(p, int):
            return p * brick
        return pl.multiple_of(p * brick, brick)

    def spread(group, c, source):
        for i in range(CHUNK):
            b = c * CHUNK + i
            p = group * nb + b
            wide[pl.ds(base_of(p), brick), :] = source(b).astype(f32)
            for y in range(rows_y):
                row = wide[pl.ds(base_of(p) + y, size, stride=rows_y), :].astype(bf16)
                near_phi[p, :, y * depth : (y + 1) * depth] = row
                if y == 0:
                    edge_send[0, p] = row
                if y == rows_y - 1:
                    edge_send[1, p] = row

    def edge_copy(side, group, c):
        piece = pl.ds(group * nb + c * CHUNK, CHUNK)
        index = group * chunks + c
        return remote(
            edge_send.at[side, piece], edge_recv.at[1 - side, piece],
            e_send.at[side, index], e_recv.at[1 - side, index],
            gy=jnp.maximum(gy - 1, 0) if side == 0 else jnp.minimum(gy + 1, n_gy - 1),
        )

    def both_sides(action):
        pl.when(has_low)(lambda: action(0))
        pl.when(has_high)(lambda: action(1))

    def own_chunk(c):
        spread(1, c, lambda b: x_ref[pl.ds(pl.multiple_of(b * brick, brick), brick), :])
        both_sides(lambda side: edge_copy(side, 1, c).start())

    def far_chunk(group, c):
        piece = pl.ds(pl.multiple_of(c * rows, rows), rows)
        remote(
            x_hbm.at[piece], raw.at[group, piece], x_send.at[group, c], x_recv.at[group, c], gx=right
        ).wait_recv()
        spread(group, c, lambda b: raw[group, pl.ds(pl.multiple_of(b * brick, brick), brick), :])
        both_sides(lambda side: edge_copy(side, group, c).start())

    def apply_chunk(group, c):
        pl.when(has_low)(lambda: edge_copy(1, group, c).wait_recv())
        pl.when(has_high)(lambda: edge_copy(0, group, c).wait_recv())
        for i in range(CHUNK):
            p = group * nb + c * CHUNK + i
            line = [edge_recv[0, p].astype(f32)]
            line += [
                near_phi[p, :, y * depth : (y + 1) * depth].astype(f32) for y in range(rows_y)
            ]
            line += [edge_recv[1, p].astype(f32)]
            for y in range(rows_y):
                center = line[y + 1]
                beside = (
                    line[y + 2] + line[y] + pltpu.roll(center, 1, 1) + pltpu.roll(center, depth - 1, 1)
                )
                applied = -0.5 * (beside - 4.0 * center) + pot_ref[y : y + 1, :] * center
                near_app[p, :, y * depth : (y + 1) * depth] = applied.astype(bf16)

    @pl.when(gy == 0)
    def _():
        edge_recv[0] = jnp.zeros(edge_recv.shape[1:], bf16)
        halo_recv[0] = jnp.zeros(halo_recv.shape[1:], bf16)

    @pl.when(gy == n_gy - 1)
    def _():
        edge_recv[1] = jnp.zeros(edge_recv.shape[1:], bf16)
        halo_recv[1] = jnp.zeros(halo_recv.shape[1:], bf16)

    first = 2 - 2 * lax.rem(gx, 2)
    second = 2 - first
    loads[0].wait()
    unrolled(chunks, own_chunk)
    for load in loads[3:]:
        load.wait()
    unrolled(chunks, lambda c: far_chunk(first, c))
    if n_gy > 2:
        k_relay(2)
    unrolled(chunks, lambda c: apply_chunk(1, c))
    for d in range(3, n_gy):
        k_relay(d)
    own_copy.wait()

    def interleaved(c):
        far_chunk(second, c)
        apply_chunk(first, c)

    unrolled(chunks, interleaved)
    unrolled(chunks, lambda c: apply_chunk(second, c))
    k_arrived(n_gy - 1)

    def picks(a):
        start = nb * n_gx + nb - nb * gx
        found = [lax.rem(cols_ref[k, a] + start, nb * n_gx) for k in range(slots)]
        return [jnp.minimum(p, 3 * nb - 1) for p in found]

    def halo_copy(side, a):
        return remote(
            halo_send.at[side, a], halo_recv.at[1 - side, a], g_send.at[side, a], g_recv.at[1 - side, a],
            gy=jnp.maximum(gy - 1, 0) if side == 0 else jnp.minimum(gy + 1, n_gy - 1),
        )

    def gradient_of(a):
        where = picks(a)
        blocks = [packs[k, a] for k in range(slots)]
        mixing = jnp.concatenate(
            [b[:, :size] for b in blocks] + [-b[:, size:] for b in blocks], axis=1
        )
        source = jnp.concatenate([near_app[p] for p in where] + [near_phi[p] for p in where], axis=0)
        total = jnp.dot(mixing, source, preferred_element_type=f32)
        for y in range(rows_y):
            piece = total[:, y * depth : (y + 1) * depth]
            grad[a, y] = piece
            if y < SWEEPS:
                halo_send[0, a, y] = piece.astype(bf16)
            if y >= rows_y - SWEEPS:
                halo_send[1, a, y - rows_y + SWEEPS] = piece.astype(bf16)
        both_sides(lambda side: halo_copy(side, a).start())

    unrolled(nb, gradient_of)

    def part_of(a):
        source = jnp.concatenate([near_app[p] for p in picks(a)], axis=0)
        block = lax.dot_general(
            near_phi[nb + a], source, (((1,), (1,)), ((), ())), preferred_element_type=f32
        ) * volume
        for k in range(slots):
            one = block[:, k * size : (k + 1) * size]
            one = jnp.concatenate([one[:half], one[half:]], axis=1)
            part[k, a] = one
            part_half[k, a] = one.astype(bf16)

    unrolled(nb, part_of)

    def part_copy(off, wide_type):
        peer = lax.rem(gy + off, n_gy)
        source, target = (part, part_recv) if wide_type else (part_half, half_recv)
        send, recv = (h_send, h_recv) if wide_type else (b_send, b_recv)
        return remote(
            source.at[pl.ds(peer * own_slots, own_slots)], target.at[off - 1],
            send.at[off - 1], recv.at[off - 1], gy=peer,
        )

    def by_distance(off, other, action):
        apart = jnp.abs(other - gy)
        pl.when(apart == 1)(lambda: action(off, True))
        pl.when(apart > 1)(lambda: action(off, False))

    for off in range(1, n_gy):
        by_distance(off, lax.rem(gy + off, n_gy), lambda o, w: part_copy(o, w).start())

    diag = 1.0 + 2.0 / kinetic_cut
    coef = 0.5 / kinetic_cut
    low, high = jnp.where(has_low, 1.0, 0.0).astype(f32), jnp.where(has_high, 1.0, 0.0).astype(f32)
    z_index = lax.broadcasted_iota(jnp.int32, (size, depth), 1)

    def finish(a):
        pl.when(has_low)(lambda: halo_copy(1, a).wait_recv())
        pl.when(has_high)(lambda: halo_copy(0, a).wait_recv())
        field = [halo_recv[0, a, i].astype(f32) for i in range(SWEEPS)]
        field += [grad[a, y] for y in range(rows_y)]
        field += [halo_recv[1, a, i].astype(f32) for i in range(SWEEPS)]
        field = [value * (1.0 / diag) for value in field]
        now = list(field)
        for sweep in range(1, SWEEPS + 1):
            later = list(now)
            for i in range(sweep, rows_y + 2 * SWEEPS - sweep):
                beside = now[i - 1] + now[i + 1]
                beside = beside + pltpu.roll(now[i], 1, 1) + pltpu.roll(now[i], depth - 1, 1)
                value = field[i] + (coef / diag) * beside
                if i < SWEEPS:
                    value = value * low
                if i >= rows_y + SWEEPS:
                    value = value * high
                later[i] = value
            now = later
        z_in = (z_index >= regs_ref[2, a]) & (z_index < regs_ref[3, a])
        for y in range(rows_y):
            spot = gy * rows_y + y
            y_in = jnp.where((spot >= regs_ref[0, a]) & (spot < regs_ref[1, a]), step_length, 0.0)
            masked = jnp.where(z_in, now[SWEEPS + y] * y_in.astype(f32), 0.0)
            phi = near_phi[nb + a, :, y * depth : (y + 1) * depth].astype(f32)
            out_ref[pl.ds(a * brick + y, size, stride=rows_y), :] = phi - masked

    unrolled(nb, finish)

    mine = pl.ds(gy * own_slots, own_slots)

    def take(off, wide_type):
        part_copy(off, wide_type).wait_recv()
        part[mine] = part[mine] + (part_recv if wide_type else half_recv)[off - 1].astype(f32)

    for off in range(1, n_gy):
        by_distance(off, lax.rem(gy + n_gy - off, n_gy), take)
    for j in range(own_slots):
        for a in range(nb):
            total = part[gy * own_slots + j, a]
            ham_ref[j, a, :half, :] = total[:, :size]
            ham_ref[j, a, half:, :] = total[:, size:]

    def sent_x(c):
        x_copy(True, c).wait_send()
        x_copy(False, c).wait_send()

    loop(chunks, sent_x)
    for group in range(3):
        loop(chunks, lambda c: both_sides(lambda side: edge_copy(side, group, c).wait_send()))
    loop(nb, lambda a: both_sides(lambda side: halo_copy(side, a).wait_send()))
    for off in range(1, n_gy):
        k_sends(off, lambda copy: copy.wait_send())
        by_distance(off, lax.rem(gy + off, n_gy), lambda o, w: part_copy(o, w).wait_send())


def store_body(support_ref, ham_ref, support_out, ham_out, sem):
    copies = [
        pltpu.make_async_copy(support_ref, support_out, sem.at[0]),
        pltpu.make_async_copy(ham_ref, ham_out, sem.at[1]),
    ]
    for copy in copies:
        copy.start()
    for copy in copies:
        copy.wait()


def local(n_gx, n_gy, support_funcs, potential, kernel, weighted, columns, regions):
    own_slots, nb, size = kernel.shape[:3]
    orbitals, rows_y, depth = support_funcs.shape
    slots = own_slots * n_gy
    flat = orbitals * rows_y
    chunks = nb // CHUNK
    vmem = pl.BlockSpec(memory_space=pltpu.VMEM)
    dma = pltpu.SemaphoreType.DMA
    operands = (
        columns.T, regions.T, potential, support_funcs.reshape(flat, depth), kernel, weighted
    )
    new_support, hamiltonian = pl.pallas_call(
        functools.partial(kernel_body, n_gx, n_gy, rows_y),
        out_shape=(
            jax.ShapeDtypeStruct((flat, depth), f32),
            jax.ShapeDtypeStruct((own_slots, nb, size, size), f32),
        ),
        in_specs=[pl.BlockSpec(memory_space=pltpu.HBM)] * 6,
        out_specs=(vmem, vmem),
        scratch_shapes=[
            pltpu.SMEM((slots, nb), jnp.int32),
            pltpu.SMEM((4, nb), jnp.int32),
            pltpu.VMEM((rows_y, depth), f32),
            pltpu.VMEM((flat, depth), bf16),
            pltpu.VMEM(kernel.shape, bf16),
            pltpu.VMEM(kernel.shape, bf16),
            pltpu.VMEM((3, flat, depth), bf16),
            pltpu.VMEM((3 * flat, depth), f32),
            pltpu.VMEM((3 * nb, size, rows_y * depth), bf16),
            pltpu.VMEM((3 * nb, size, rows_y * depth), bf16),
            pltpu.VMEM((2, 3 * nb, size, depth), bf16),
            pltpu.VMEM((2, 3 * nb, size, depth), bf16),
            pltpu.VMEM((own_slots, nb, size, 2 * size), bf16),
            pltpu.VMEM((slots, nb, size, 2 * size), bf16),
            pltpu.VMEM((nb, rows_y, size, depth), f32),
            pltpu.VMEM((2, nb, SWEEPS, size, depth), bf16),
            pltpu.VMEM((2, nb, SWEEPS, size, depth), bf16),
            pltpu.VMEM((slots, nb, size // 2, 2 * size), f32),
            pltpu.VMEM((slots, nb, size // 2, 2 * size), bf16),
            pltpu.VMEM((n_gy - 1, own_slots, nb, size // 2, 2 * size), f32),
            pltpu.VMEM((n_gy - 1, own_slots, nb, size // 2, 2 * size), bf16),
            dma((6,)),
            dma((3, chunks)),
            dma((3, chunks)),
            dma((2, 3 * chunks)),
            dma((2, 3 * chunks)),
            dma((2, n_gy - 1)),
            dma((2, n_gy - 1)),
            dma(()),
            dma((2, nb)),
            dma((2, nb)),
            dma((n_gy - 1,)),
            dma((n_gy - 1,)),
            dma((n_gy - 1,)),
            dma((n_gy - 1,)),
        ],
        compiler_params=pltpu.CompilerParams(
            collective_id=0, has_side_effects=True, vmem_limit_bytes=40 * 1024 * 1024
        ),
    )(*[pltpu.with_memory_space_constraint(v, pltpu.HBM) for v in operands])
    hbm = pl.BlockSpec(memory_space=pltpu.HBM)
    new_support, hamiltonian = pl.pallas_call(
        store_body,
        out_shape=(
            jax.ShapeDtypeStruct(new_support.shape, f32),
            jax.ShapeDtypeStruct(hamiltonian.shape, f32),
        ),
        in_specs=[vmem, vmem],
        out_specs=(hbm, hbm),
        scratch_shapes=[dma((2,))],
        compiler_params=pltpu.CompilerParams(vmem_limit_bytes=8 * 1024 * 1024),
    )(new_support, hamiltonian)
    return (new_support.reshape(orbitals, rows_y, depth), hamiltonian)


def solution(mesh):
    return jax.shard_map(
        functools.partial(local, mesh.shape["gx"], mesh.shape["gy"]),
        mesh=mesh,
        in_specs=(
            P("gx", "gy", None),
            P("gy", None),
            P("gy", "gx", None, None),
            P("gy", "gx", None, None),
            P("gx", None),
            P("gx", None),
        ),
        out_specs=(P("gx", "gy", None), P("gy", "gx", None, None)),
        check_vma=False,
    )
```
